32 devices in a mesh: parts: 2 (over x), space: 16 (over z, y, core).
Axes of the slice: x: 2, y: 2, z: 4, core: 2. Of those that a mesh axis runs over, the one named last changes fastest.
Arguments:
- images: bfloat16 [8, 32, 128, 512], P('parts', 'space'), parts along dimension 0, may hold values from 0 to 0.099609375
- target: bfloat16 [8, 16, 64, 1024], P('parts', 'space'), parts along dimension 0, may hold values from -8 to 8
- raw_filters: bfloat16 [2048, 3, 3, 512], P(('parts', 'space')), parts along dimension 0, may hold values from -39 to 39
Outputs:
- input_grads: bfloat16 [8, 32, 128, 512], P('parts', 'space'), parts along dimension 0
- filter_grads: float32 [2048, 3, 3, 512], P(('parts', 'space')), parts along dimension 0
The draws below stay inside these ranges and needn't reach their ends.
There are 2 independent parts, one for each index of `parts`. The reference program is written for one: setup_inputs(seed, part) draws one part's arguments, and reference() takes and returns one part's arrays. A program takes and returns all parts, laid end to end along the dimension named above; each array names one. Nothing has to cross between parts.
All inputs are finite; a program needn't handle non-finite values.
Results may differ from the reference program's by a relative error of at most 0.008.
Values may be sent and summed in bfloat16 or wider, within the bound.
A program may use at most 128 MiB of HBM per device.

```python
import math
import jax
import jax.numpy as jnp
from jax import lax

CIN = 512
COUT = 1024
IMG = 4
WO = 64
OUT_ROWS = 16
IN_ROWS = 32
IN_COLS = 128


def draw_raw_filters(key, part):
    keys = jax.random.split(key, 4)
    shape = (COUT, 3, 3, CIN)
    noise = jax.random.truncated_normal(keys[0], -4.0, 4.0, shape, jnp.float32)
    row_scale = jnp.exp(jax.random.uniform(keys[1], (COUT, 1, 1, 1), jnp.float32, math.log(0.3), math.log(3.0)))
    col_scale = jnp.exp(jax.random.uniform(keys[2], (1, 1, 1, CIN), jnp.float32, math.log(0.3), math.log(3.0)))
    offset = jax.random.uniform(keys[3], (COUT, 1, 1, 1), jnp.float32, -1.0, 1.0) * row_scale
    return (noise * row_scale * col_scale + offset).astype(jnp.bfloat16)


def level_of(own_key, extent, cuts, smallest, top_value):
    def one(position, shards_of):
        draws = jax.random.uniform(jax.random.fold_in(jax.random.fold_in(own_key, 6), position), (shards_of,), jnp.float32, smallest / len(cuts), top_value / len(cuts))
        return jnp.repeat(jnp.exp(draws), extent[position] // shards_of).reshape((-1,) + (1,) * (len(extent) - position - 1))

    gain = one(*cuts[0])
    for cut in cuts[1:]:
        gain = gain * one(*cut)
    return gain


def gaussian(own_key, dims, scale, limit, cuts=(), kind=jnp.bfloat16):
    gain = level_of(own_key, dims, cuts, -0.22, 0.18) if cuts else 1.0
    entries = jax.random.normal(own_key, dims, jnp.float32) * scale * gain
    return jnp.minimum(jnp.maximum(entries, -limit), limit).astype(kind)


def setup_inputs(seed: int = 0, part: int = 0) -> dict:
    key_of = jax.random.split(jax.random.key(seed), 4)
    part_keys = jax.random.split(jax.random.fold_in(key_of[3], part), 4)
    images = jnp.clip(0.099609375 * jax.random.uniform(part_keys[0], (IMG, IN_ROWS, IN_COLS, CIN), jnp.float32) ** level_of(part_keys[0], (IMG, IN_ROWS, IN_COLS, CIN), ((1, 16),), -0.2, 0.2), 0.0, 0.099609375).astype(jnp.bfloat16)
    target = gaussian(part_keys[1], (IMG, OUT_ROWS, WO, COUT), 2.0, 8.0, ((1, 16),))
    raw_filters = draw_raw_filters(jax.random.fold_in(jax.random.fold_in(key_of[3], part), 71), part)
    return dict(images=images, target=target, raw_filters=raw_filters)


EPS = 1e-05
GRAD_SCALE = 0.015625

def extract(padded):
    pieces = []
    for kh in range(3):
        for kw in range(3):
            pieces.append(padded[:, kh:kh + 2 * OUT_ROWS:2, kw:kw + 2 * WO:2, :])
    return jnp.concatenate(pieces, axis=-1)

def reference(images, target, raw_filters):
    weights = raw_filters.astype(jnp.float32).reshape(COUT, 9 * CIN)
    mean_w = lax.optimization_barrier(jnp.mean(weights, axis=1, keepdims=True))
    centered = weights - mean_w
    std_w = jnp.sqrt(lax.optimization_barrier(jnp.mean(centered * centered, axis=1, keepdims=True)) + EPS)
    w_hat = centered / std_w
    w_bf = w_hat.astype(jnp.bfloat16)
    padded = jnp.pad(images, ((0, 0), (1, 1), (1, 1), (0, 0)))
    patches = extract(padded).reshape(IMG * OUT_ROWS * WO, 9 * CIN)
    outputs = jnp.dot(patches, w_bf.T, preferred_element_type=jnp.float32)
    wanted = target.reshape(IMG * OUT_ROWS * WO, COUT).astype(jnp.float32)
    grad_y = ((outputs - wanted) * GRAD_SCALE).astype(jnp.bfloat16)
    summed = jnp.dot(grad_y.T, patches, preferred_element_type=jnp.float32)
    first_mean = lax.optimization_barrier(jnp.mean(summed, axis=1, keepdims=True))
    second_mean = lax.optimization_barrier(jnp.mean(summed * w_hat, axis=1, keepdims=True))
    filter_grads = ((summed - first_mean - w_hat * second_mean) / std_w).reshape(COUT, 3, 3, CIN)
    columns = jnp.dot(grad_y, w_bf, preferred_element_type=jnp.float32)
    columns = columns.reshape(IMG, OUT_ROWS, WO, 9 * CIN)
    start_field = jnp.zeros(padded.shape, jnp.float32)
    unused, backward = jax.vjp(extract, start_field)
    spread_back = backward(columns)[0]
    input_grads = spread_back[:, 1:-1, 1:-1, :].astype(jnp.bfloat16)
    return (input_grads, filter_grads)
```

```python
import jax
import jax.numpy as jnp
from jax import lax
from jax.sharding import PartitionSpec as P

EPS = 1e-05
GRAD_SCALE = 0.015625
GROUP = 4


def standardize(rows):
    values = rows.astype(jnp.float32)
    centre = jnp.mean(values, axis=1, keepdims=True)
    shifted = values - centre
    spread = jnp.sqrt(jnp.mean(shifted * shifted, axis=1, keepdims=True) + EPS)
    return (shifted / spread, spread)


def dot(a, b, dims):
    return lax.dot_general(a, b, (dims, ((), ())), preferred_element_type=jnp.float32)


def shards(images, target, raw_filters):
    count_img, two_rows, in_cols, cin = images.shape
    half = in_cols // 2
    own_count = raw_filters.shape[0]
    devices = lax.axis_size("space")
    wide = GROUP if devices % GROUP == 0 else 1
    tall = devices // wide
    near = [[r * wide + f for f in range(wide)] for r in range(tall)]
    far = [[r * wide + f for r in range(tall)] for f in range(wide)]
    fan = 9 * cin
    bf = jnp.bfloat16
    pair = images.reshape(count_img, two_rows, half, 2 * cin)
    own_hat, own_spread = standardize(raw_filters.reshape(own_count, fan))
    rows_bf = lax.all_gather(own_hat.astype(bf), "space", axis_index_groups=far, tiled=True)
    tiles = lax.all_gather(pair, "space", axis_index_groups=near)
    wanted = target.reshape(count_img, half, tall, wide, own_count)
    wanted = lax.all_to_all(
        wanted, "space", 3, 0, axis_index_groups=near, tiled=False
    )
    wanted = wanted.reshape(wide, count_img * half, tall * own_count)
    route = [(i, i + wide) for i in range(devices - wide)]
    last = lax.ppermute(tiles[-1, :, 1], "space", route)
    filters = tall * own_count
    rows = jnp.concatenate(
        [last[None, :], tiles.transpose(0, 2, 1, 3, 4).reshape(2 * wide, count_img, half, 2 * cin)],
        axis=0,
    )
    odd = rows[..., cin:]
    before = jnp.pad(odd[:, :, :-1], ((0, 0), (0, 0), (1, 0), (0, 0)))
    full = jnp.concatenate([before, rows], axis=-1).reshape(2 * wide + 1, count_img * half, 3 * cin)
    patches = jnp.concatenate([full[k : k + 2 * wide : 2] for k in range(3)], axis=-1)
    patches = patches.reshape(wide * count_img * half, fan)
    block = dot(patches, rows_bf, ((1,), (1,)))
    goal = wanted.reshape(wide * count_img * half, filters).astype(jnp.float32)
    grad = ((block - goal) * GRAD_SCALE).astype(bf)
    part = dot(grad, patches, ((0,), (0,)))
    summed = lax.psum_scatter(
        part.astype(bf), "space", axis_index_groups=far, tiled=True
    ).astype(jnp.float32)
    columns = dot(grad, rows_bf, ((1,), (0,))).reshape(wide, count_img, half, 3, 3, cin)
    later = jnp.pad(columns[:, :, 1:, :, 0], ((0, 0), (0, 0), (0, 1), (0, 0), (0, 0)))
    odds = columns[:, :, :, :, 2] + later
    both = jnp.concatenate([columns[:, :, :, :, 1], odds], axis=-1)
    upper, middle, lower = both[:, :, :, 0], both[:, :, :, 1], both[:, :, :, 2]
    lower = lower + jnp.concatenate([upper[1:], jnp.zeros_like(upper[:1])], axis=0)
    inner = jnp.stack([middle, lower], axis=1).astype(bf)
    mine = lax.psum_scatter(inner, "space", axis_index_groups=near, tiled=False)
    back = [(i + wide, i) for i in range(devices - wide)]
    edge = lax.ppermute(upper[0].astype(bf), "space", back)
    edge = lax.psum_scatter(
        jnp.stack([jnp.zeros_like(edge)] * (wide - 1) + [edge]), "space", axis_index_groups=near, tiled=False
    )
    low = (mine[1].astype(jnp.float32) + edge.astype(jnp.float32)).astype(bf)
    input_grads = jnp.stack([mine[0], low], axis=1).reshape(images.shape)
    first_mean = jnp.mean(summed, axis=1, keepdims=True)
    second_mean = jnp.mean(summed * own_hat, axis=1, keepdims=True)
    filter_grads = ((summed - first_mean - own_hat * second_mean) / own_spread).reshape(
        raw_filters.shape
    )
    return (input_grads, filter_grads)


def solution(mesh):
    return jax.shard_map(
        shards,
        mesh=mesh,
        in_specs=(
            P("parts", "space", None, None),
            P("parts", "space", None, None),
            P(("parts", "space"), None, None, None),
        ),
        out_specs=(P("parts", "space", None, None), P(("parts", "space"), None, None, None)),
        check_vma=False,
    )
```

```python
import functools

import jax
import jax.numpy as jnp
from jax import lax
from jax.experimental import pallas as pl
from jax.experimental.pallas import tpu as pltpu
from jax.sharding import PartitionSpec as P

EPS = 1e-05
GRAD_SCALE = 0.015625
WIDE = 4
F32 = jnp.float32
BF = jnp.bfloat16
NT = (((1,), (1,)), ((), ()))
NN = (((1,), (0,)), ((), ()))


def standardize(rows):
    values = rows.astype(F32)
    centre = jnp.mean(values, axis=1, keepdims=True)
    shifted = values - centre
    spread = jnp.sqrt(jnp.mean(shifted * shifted, axis=1, keepdims=True) + EPS)
    return (shifted / spread, spread)


def dot(a, b, dims):
    return lax.dot_general(a, b, dims, preferred_element_type=F32)


def kernel(
    tall, own, half, cin,
    pair, goal, hat, dout, gout,
    x, w, tg, gy, gys, gt, gts, g,
    up_in, dn_in, up_out, dn_out,
    to_p, from_p, to_q, from_q, acc, rim_s, rim_p, rim_q, rim_z,
    x_recv, x_send, w_recv, w_up, w_dn, t_recv, t_send, r_recv, r_send,
    gu_recv, gu_send, gd_recv, gd_send, d_recv, d_send, e_recv, e_send,
):
    me = lax.axis_index("space")
    r, f = me // WIDE, me % WIDE
    base = r * WIDE
    fp = f + 1 - 2 * (f % 2)
    fq = f + 2 - 4 * (f // 2)
    fd = fp + 2 - 4 * (fp // 2)
    p, q, d = base + fp, base + fq, base + fd
    above, below = me - WIDE, me + WIDE
    px = pair.shape[1]
    two, one = 2 * cin, cin
    three = 3 * cin

    def rc(src, dst, ssem, rsem, to):
        return pltpu.make_async_remote_copy(
            src_ref=src, dst_ref=dst, send_sem=ssem, recv_sem=rsem,
            device_id={"space": to}, device_id_type=pl.DeviceIdType.MESH,
        )

    def wait_in(dst, rsem):
        rc(dst, dst, rsem, rsem, p).wait_recv()

    bar = pltpu.get_barrier_semaphore()

    def greet(to):
        pl.semaphore_signal(bar, inc=1, device_id={"space": to}, device_id_type=pl.DeviceIdType.MESH)

    for to in (p, q, d):
        greet(to)

    @pl.when(r > 0)
    def _():
        greet(above)

    @pl.when(r < tall - 1)
    def _():
        greet(below)

    inside = (r > 0) & (r < tall - 1)

    @pl.when(inside)
    def _():
        pl.semaphore_wait(bar, 5)

    @pl.when(jnp.logical_not(inside))
    def _():
        pl.semaphore_wait(bar, 4)

    def own_rows(b):
        return pl.ds(pl.multiple_of(b * own, own), own)

    def img_copy(row, k, to):
        slot = x.at[1 + 2 * f + row]
        return rc(pair.at[row], slot, x_send.at[k, row], x_recv.at[f, row], to)

    def fwd_copy(row):
        slot = x.at[1 + 2 * fq + row]
        return rc(slot, slot, x_send.at[2, row], x_recv.at[fq, row], p)

    def tgt_copy(k, to_f, to):
        return rc(goal.at[to_f], tg.at[f], t_send.at[k], t_recv.at[f], to)

    def w_copy(b, first, sem, to):
        slot = w.at[own_rows(b)]
        return rc(hat if first else slot, slot, sem.at[b], w_recv.at[b], to)

    rim_in = rc(pair.at[1], x.at[0], r_send.at[0], r_recv, below)
    rim_to_p = rc(x.at[0], x.at[0], r_send.at[1], r_recv, p)
    rim_to_q = rc(x.at[0], x.at[0], r_send.at[2], r_recv, q)

    def filters_step(s):
        b_up, b_dn = r - s, r + s

        @pl.when(b_up >= 0)
        def _():
            if s > 0:
                wait_in(w.at[own_rows(b_up)], w_recv.at[b_up])

            @pl.when(r < tall - 1)
            def _():
                w_copy(b_up, s == 0, w_up, below).start()

        @pl.when(b_dn <= tall - 1)
        def _():
            if s > 0:
                wait_in(w.at[own_rows(b_dn)], w_recv.at[b_dn])

            @pl.when(r > 0)
            def _():
                w_copy(b_dn, s == 0, w_dn, above).start()

    @pl.when((f == 3) & (r < tall - 1))
    def _():
        rim_in.start()

    filters_step(0)
    for row in range(2):
        img_copy(row, 1, q).start()
    for row in range(2):
        img_copy(row, 0, p).start()
    tgt_copy(0, fp, p).start()
    tgt_copy(1, fq, q).start()
    tgt_copy(2, fd, d).start()
    for row in range(2):
        x[1 + 2 * f + row] = pair[row]
    w[own_rows(r)] = hat[...]
    tg[f] = goal[f]

    def forward_row(row):
        wait_in(x.at[1 + 2 * fq + row], x_recv.at[fq, row])
        fwd_copy(row).start()

    def rim_step():
        @pl.when(r > 0)
        def _():
            wait_in(x.at[0], r_recv)

            @pl.when(f == 3)
            def _():
                rim_to_q.start()

            @pl.when(f % 2 == 1)
            def _():
                rim_to_p.start()

        @pl.when(r == 0)
        def _():
            x[0] = jnp.zeros((px, two), BF)

    for s in range(1, tall):
        filters_step(s)
        if s == 1:
            forward_row(0)
            rim_step()
        if s == 2:
            forward_row(1)
    for row in range(2):
        wait_in(x.at[1 + 2 * fp + row], x_recv.at[fp, row])
        wait_in(x.at[1 + 2 * fd + row], x_recv.at[fd, row])
    for t in (fp, fq, fd):
        wait_in(tg.at[t], t_recv.at[t])

    filters = tall * own
    place = lax.broadcasted_iota(jnp.int32, (px, filters), 0) % half
    gy[WIDE] = jnp.zeros((px, filters), BF)
    gys[WIDE] = jnp.zeros((px, filters), BF)

    def forward(t, carry):
        both = jnp.zeros((px, filters), F32)
        left = jnp.zeros((px, filters), F32)
        for kh in range(3):
            c = kh * three
            both += dot(x[2 * t + kh], w[:, c + one : c + three], NT)
            left += dot(x[2 * t + kh, :, one:two], w[:, c : c + one], NT)
        out = both + jnp.where(place == 0, 0.0, pltpu.roll(left, 1, 0))
        grad = ((out - tg[t].astype(F32)) * GRAD_SCALE).astype(BF)
        wide = grad.astype(F32)
        ahead = jnp.where(place == half - 1, 0.0, pltpu.roll(wide, px - 1, 0))
        gy[t] = grad
        gys[t] = ahead.astype(BF)
        gt[t] = wide.T.astype(BF)
        gts[t] = ahead.T.astype(BF)
        return carry

    lax.fori_loop(0, WIDE, forward, 0)

    for kh in range(3):
        c = kh * three
        for n in range(3):
            lanes = slice(c + n * one, c + (n + 1) * one)
            src = slice(0, one) if n == 1 else slice(one, two)
            lhs = gts if n == 0 else gt
            total = dot(lhs[0], x[kh, :, src], NN)
            for t in range(1, WIDE):
                total += dot(lhs[t], x[2 * t + kh, :, src], NN)
            g[:, lanes] = total

    def centre(b, carry):
        block = g[own_rows(b)]
        g[own_rows(b)] = block - jnp.mean(block, axis=1, keepdims=True)
        return carry

    lax.fori_loop(0, tall, centre, 0)

    def up_copy(b):
        return rc(up_out.at[own_rows(b)], up_in.at[own_rows(b)], gu_send.at[b], gu_recv.at[b], below)

    def dn_copy(b):
        return rc(dn_out.at[own_rows(b)], dn_in.at[own_rows(b)], gd_send.at[b], gd_recv.at[b], above)

    for s in range(tall - 1):
        b = tall - 1 - s

        @pl.when(r == 0)
        def _():
            up_out[own_rows(b)] = g[own_rows(b)].astype(BF)
            up_copy(b).start()

        @pl.when(r == tall - 1)
        def _():
            dn_out[own_rows(s)] = g[own_rows(s)].astype(BF)
            dn_copy(s).start()

    def relay(s):
        b = tall - 1 - s

        @pl.when((r > 0) & (b > r))
        def _():
            wait_in(up_in.at[own_rows(b)], gu_recv.at[b])
            up_out[own_rows(b)] = (g[own_rows(b)] + up_in[own_rows(b)].astype(F32)).astype(BF)
            up_copy(b).start()

        @pl.when((r < tall - 1) & (s < r))
        def _():
            wait_in(dn_in.at[own_rows(s)], gd_recv.at[s])
            dn_out[own_rows(s)] = (g[own_rows(s)] + dn_in[own_rows(s)].astype(F32)).astype(BF)
            dn_copy(s).start()

    def taps(t, kh):
        c = kh * three
        even = dot(gy[t], w[:, c + one : c + two], NN)
        odd = dot(gy[t], w[:, c + two : c + three], NN)
        odd += dot(gys[t], w[:, c : c + one], NN)
        return even, odd

    def tile_row(t, row):
        if row == 0:
            return taps(t, 1)
        even, odd = taps(t, 2)
        more_even, more_odd = taps(t + 1, 0)
        return even + more_even, odd + more_odd

    halves = (slice(0, one), slice(one, two))
    rim_pc = rc(rim_s, rim_p, e_send, e_recv.at[0], p)
    rim_qc = rc(rim_s, rim_q, e_send, e_recv.at[1], q)
    rim_zc = rc(rim_s, rim_z, e_send, e_recv.at[2], above)

    @pl.when(r > 0)
    def _():
        edge = taps(0, 0)
        for part, lanes in zip(edge, halves):
            acc[0, :, lanes] = part

        @pl.when(f % 2 == 0)
        def _():
            rim_s[...] = acc[0].astype(BF)
            rim_pc.start()

    def p_copy(k):
        return rc(to_p.at[k], from_p.at[k], d_send.at[k], d_recv.at[k], p)

    for k in (1, 0):
        t = fd if k else fp
        for row in range(2):
            for part, lanes in zip(tile_row(t, row), halves):
                to_p[k, row, :, lanes] = part.astype(BF)
        p_copy(k).start()

    @pl.when((r > 0) & (f == 1))
    def _():
        wait_in(rim_p, e_recv.at[0])
        rim_s[...] = (acc[0] + rim_p[...].astype(F32)).astype(BF)
        rim_qc.start()

    @pl.when((r > 0) & (f == 3))
    def _():
        wait_in(rim_p, e_recv.at[0])
        wait_in(rim_q, e_recv.at[1])
        rim_s[...] = (acc[0] + rim_p[...].astype(F32) + rim_q[...].astype(F32)).astype(BF)
        rim_zc.start()

    q_copy = rc(to_q, from_q, d_send.at[2], d_recv.at[2], q)
    wait_in(from_p.at[1], d_recv.at[1])
    for row in range(2):
        for part, lanes in zip(tile_row(fq, row), halves):
            to_q[row, :, lanes] = (part + from_p[1, row, :, lanes].astype(F32)).astype(BF)
    q_copy.start()
    for row in range(2):
        for part, lanes in zip(tile_row(f, row), halves):
            acc[row, :, lanes] = part
    for s in range(tall - 1):
        relay(s)

    wait_in(from_p.at[0], d_recv.at[0])
    wait_in(from_q, d_recv.at[2])
    for row in range(2):
        acc[row] += from_p[0, row].astype(F32) + from_q[row].astype(F32)

    @pl.when((r < tall - 1) & (f == 3))
    def _():
        wait_in(rim_z, e_recv.at[2])
        acc[1] += rim_z[...].astype(F32)

    for row in range(2):
        dout[row] = acc[row].astype(BF)

    gout[...] = g[own_rows(r)]

    @pl.when(r > 0)
    def _():
        wait_in(up_in.at[own_rows(r)], gu_recv.at[r])
        gout[...] += up_in[own_rows(r)].astype(F32)

    @pl.when(r < tall - 1)
    def _():
        wait_in(dn_in.at[own_rows(r)], gd_recv.at[r])
        gout[...] += dn_in[own_rows(r)].astype(F32)

    for row in range(2):
        img_copy(row, 0, p).wait_send()
        img_copy(row, 1, q).wait_send()
        fwd_copy(row).wait_send()
    tgt_copy(0, fp, p).wait_send()
    tgt_copy(1, fq, q).wait_send()
    tgt_copy(2, fd, d).wait_send()
    p_copy(0).wait_send()
    p_copy(1).wait_send()
    q_copy.wait_send()

    @pl.when((f == 3) & (r < tall - 1))
    def _():
        rim_in.wait_send()

    @pl.when((r > 0) & (f == 3))
    def _():
        rim_to_q.wait_send()

    @pl.when((r > 0) & (f % 2 == 1))
    def _():
        rim_to_p.wait_send()

    @pl.when(r > 0)
    def _():
        rim_pc.wait_send()

    for b in range(tall):
        @pl.when((r < tall - 1) & (b <= r))
        def _():
            w_copy(b, False, w_up, below).wait_send()

        @pl.when((r > 0) & (b >= r))
        def _():
            w_copy(b, False, w_dn, above).wait_send()

        @pl.when(b > r)
        def _():
            up_copy(b).wait_send()

        @pl.when(b < r)
        def _():
            dn_copy(b).wait_send()


def shards(images, target, raw_filters):
    count_img, two_rows, in_cols, cin = images.shape
    half = in_cols // 2
    own = raw_filters.shape[0]
    tall = lax.axis_size("space") // WIDE
    fan = 9 * cin
    px = count_img * half
    filters = tall * own
    own_hat, own_spread = standardize(raw_filters.reshape(own, fan))
    pair = images.reshape(count_img, two_rows, half, 2 * cin).transpose(1, 0, 2, 3)
    pair = pair.reshape(two_rows, px, 2 * cin)
    goal = target.reshape(px, tall, WIDE, own).transpose(2, 0, 1, 3).reshape(WIDE, px, filters)
    vm = pltpu.VMEM
    dma = pltpu.SemaphoreType.DMA
    row = (px, 2 * cin)
    scratch = [
        vm((2 * WIDE + 1,) + row, BF), vm((filters, fan), BF), vm((WIDE, px, filters), BF),
        vm((WIDE + 1, px, filters), BF), vm((WIDE + 1, px, filters), BF),
        vm((WIDE, filters, px), BF), vm((WIDE, filters, px), BF), vm((filters, fan), F32),
        vm((filters, fan), BF), vm((filters, fan), BF), vm((filters, fan), BF), vm((filters, fan), BF),
        vm((2, 2) + row, BF), vm((2, 2) + row, BF), vm((2,) + row, BF), vm((2,) + row, BF),
        vm((2,) + row, F32), vm(row, BF), vm(row, BF), vm(row, BF), vm(row, BF),
        dma((WIDE, 2)), dma((3, 2)), dma((tall,)), dma((tall,)), dma((tall,)),
        dma((WIDE,)), dma((3,)), dma, dma((3,)),
        dma((tall,)), dma((tall,)), dma((tall,)), dma((tall,)), dma((3,)), dma((3,)), dma((3,)), dma,
    ]
    inner, summed = pl.pallas_call(
        functools.partial(kernel, tall, own, half, cin),
        out_shape=(
            jax.ShapeDtypeStruct((2,) + row, BF),
            jax.ShapeDtypeStruct((own, fan), F32),
        ),
        in_specs=[pl.BlockSpec(memory_space=pltpu.VMEM)] * 3,
        out_specs=[pl.BlockSpec(memory_space=pltpu.VMEM)] * 2,
        scratch_shapes=scratch,
        compiler_params=pltpu.CompilerParams(
            collective_id=0, has_side_effects=True, vmem_limit_bytes=60 * 1024 * 1024
        ),
        name="tiles",
    )(pair, goal, own_hat.astype(BF))
    input_grads = inner.reshape(2, count_img, half, 2 * cin).transpose(1, 0, 2, 3).reshape(images.shape)
    first_mean = jnp.mean(summed, axis=1, keepdims=True)
    second_mean = jnp.mean(summed * own_hat, axis=1, keepdims=True)
    filter_grads = ((summed - first_mean - own_hat * second_mean) / own_spread).reshape(
        raw_filters.shape
    )
    return (input_grads, filter_grads)


def solution(mesh):
    return jax.shard_map(
        shards,
        mesh=mesh,
        in_specs=(
            P("parts", "space", None, None),
            P("parts", "space", None, None),
            P(("parts", "space"), None, None, None),
        ),
        out_specs=(P("parts", "space", None, None), P(("parts", "space"), None, None, None)),
        check_vma=False,
    )
```

```python
import functools

import jax
import jax.numpy as jnp
from jax import lax
from jax.experimental import pallas as pl
from jax.experimental.pallas import tpu as pltpu
from jax.sharding import PartitionSpec as P

EPS = 1e-05
GRAD_SCALE = 0.015625
WIDE = 4
F32 = jnp.float32
BF = jnp.bfloat16
NT = (((1,), (1,)), ((), ()))
NN = (((1,), (0,)), ((), ()))


def standardize(rows):
    values = rows.astype(F32)
    centre = jnp.mean(values, axis=1, keepdims=True)
    shifted = values - centre
    spread = jnp.sqrt(jnp.mean(shifted * shifted, axis=1, keepdims=True) + EPS)
    return (shifted / spread, spread)


def dot(a, b, dims):
    return lax.dot_general(a, b, dims, preferred_element_type=F32)


def kernel(
    tall, own, half, cin,
    pair, goal, hat, dout, gout,
    x, w, tg, gy, gys, gt, gts, g,
    up_in, dn_in, up_out, dn_out,
    to_p, from_p, to_q, from_q, acc, rim_s, rim_p, rim_q, rim_z,
    x_recv, x_send, w_recv, w_up, w_dn, t_recv, t_send, r_recv, r_send,
    gu_recv, gu_send, gd_recv, gd_send, d_recv, d_send, e_recv, e_send,
):
    me = lax.axis_index("space")
    r, f = me // WIDE, me % WIDE
    base = r * WIDE
    fp = f + 1 - 2 * (f % 2)
    fq = f + 2 - 4 * (f // 2)
    fd = fp + 2 - 4 * (fp // 2)
    p, q, d = base + fp, base + fq, base + fd
    above, below = me - WIDE, me + WIDE
    imgs = pair.shape[0]
    px = imgs * half
    two, one = 2 * cin, cin
    three = 3 * cin

    def rc(src, dst, ssem, rsem, to):
        return pltpu.make_async_remote_copy(
            src_ref=src, dst_ref=dst, send_sem=ssem, recv_sem=rsem,
            device_id={"space": to}, device_id_type=pl.DeviceIdType.MESH,
        )

    def wait_in(dst, rsem):
        rc(dst, dst, rsem, rsem, p).wait_recv()

    bar = pltpu.get_barrier_semaphore()

    def greet(to):
        pl.semaphore_signal(bar, inc=1, device_id={"space": to}, device_id_type=pl.DeviceIdType.MESH)

    for to in (p, q, d):
        greet(to)

    @pl.when(r > 0)
    def _():
        greet(above)

    @pl.when(r < tall - 1)
    def _():
        greet(below)

    inside = (r > 0) & (r < tall - 1)

    @pl.when(inside)
    def _():
        pl.semaphore_wait(bar, 5)

    @pl.when(jnp.logical_not(inside))
    def _():
        pl.semaphore_wait(bar, 4)

    def own_rows(b):
        return pl.ds(pl.multiple_of(b * own, own), own)

    def img_copy(row, k, to):
        slot = x.at[1 + 2 * f + row]
        return rc(pair.at[:, row], slot, x_send.at[k, row], x_recv.at[f, row], to)

    def fwd_copy(row):
        slot = x.at[1 + 2 * fq + row]
        return rc(slot, slot, x_send.at[2, row], x_recv.at[fq, row], p)

    def tgt_copy(k, to_f, to):
        return rc(goal.at[to_f], tg.at[f], t_send.at[k], t_recv.at[f], to)

    def w_copy(b, first, sem, to):
        slot = w.at[own_rows(b)]
        return rc(hat if first else slot, slot, sem.at[b], w_recv.at[b], to)

    rim_in = rc(pair.at[:, 1], x.at[0], r_send.at[0], r_recv, below)
    rim_to_p = rc(x.at[0], x.at[0], r_send.at[1], r_recv, p)
    rim_to_q = rc(x.at[0], x.at[0], r_send.at[2], r_recv, q)

    def filters_step(s):
        b_up, b_dn = r - s, r + s

        @pl.when(b_up >= 0)
        def _():
            if s > 0:
                wait_in(w.at[own_rows(b_up)], w_recv.at[b_up])

            @pl.when(r < tall - 1)
            def _():
                w_copy(b_up, s == 0, w_up, below).start()

        @pl.when(b_dn <= tall - 1)
        def _():
            if s > 0:
                wait_in(w.at[own_rows(b_dn)], w_recv.at[b_dn])

            @pl.when(r > 0)
            def _():
                w_copy(b_dn, s == 0, w_dn, above).start()

    @pl.when((f == 3) & (r < tall - 1))
    def _():
        rim_in.start()

    filters_step(0)
    for row in range(2):
        img_copy(row, 1, q).start()
    for row in range(2):
        img_copy(row, 0, p).start()
    tgt_copy(0, fp, p).start()
    tgt_copy(1, fq, q).start()
    tgt_copy(2, fd, d).start()
    for row in range(2):
        x[1 + 2 * f + row] = pair[:, row]
    w[own_rows(r)] = hat[...]
    tg[f] = goal[f]

    def forward_row(row):
        wait_in(x.at[1 + 2 * fq + row], x_recv.at[fq, row])
        fwd_copy(row).start()

    def rim_step():
        @pl.when(r > 0)
        def _():
            wait_in(x.at[0], r_recv)

            @pl.when(f == 3)
            def _():
                rim_to_q.start()

            @pl.when(f % 2 == 1)
            def _():
                rim_to_p.start()

        @pl.when(r == 0)
        def _():
            x[0] = jnp.zeros((imgs, half, two), BF)

    for s in range(1, tall - 1):
        filters_step(s)
        if s == 1:
            forward_row(0)
            rim_step()
        if s == 2:
            forward_row(1)
    for row in range(2):
        wait_in(x.at[1 + 2 * fp + row], x_recv.at[fp, row])
        wait_in(x.at[1 + 2 * fd + row], x_recv.at[fd, row])
    for t in (fp, fq, fd):
        wait_in(tg.at[t], t_recv.at[t])

    filters = tall * own
    hf, mid = filters // 2, tall // 2
    own_half = r // mid
    place = lax.broadcasted_iota(jnp.int32, (px, hf), 0) % half
    gy[WIDE] = jnp.zeros((px, filters), BF)
    gys[WIDE] = jnp.zeros((px, filters), BF)

    def img(index, lanes):
        return x[index, :, :, lanes].reshape(px, lanes.stop - lanes.start)

    def forward(h, t):
        part = pl.ds(pl.multiple_of(h * hf, hf), hf)
        both = jnp.zeros((px, hf), F32)
        left = jnp.zeros((px, hf), F32)
        for kh in range(3):
            c = kh * three
            both += dot(img(2 * t + kh, slice(0, two)), w[part, c + one : c + three], NT)
            left += dot(img(2 * t + kh, slice(one, two)), w[part, c : c + one], NT)
        out = both + jnp.where(place == 0, 0.0, pltpu.roll(left, 1, 0))
        grad = ((out - tg[t, :, part].astype(F32)) * GRAD_SCALE).astype(BF)
        wide = grad.astype(F32)
        ahead = jnp.where(place == half - 1, 0.0, pltpu.roll(wide, px - 1, 0))
        gy[t, :, part] = grad
        gys[t, :, part] = ahead.astype(BF)
        gt[t, part] = wide.T.astype(BF)
        gts[t, part] = ahead.T.astype(BF)

    def filter_terms(h):
        part = pl.ds(pl.multiple_of(h * hf, hf), hf)
        for kh in range(3):
            c = kh * three
            for n in range(3):
                lanes = slice(c + n * one, c + (n + 1) * one)
                src = slice(0, one) if n == 1 else slice(one, two)
                lhs = gts if n == 0 else gt
                total = dot(lhs[0, part], img(kh, src), NN)
                for t in range(1, WIDE):
                    total += dot(lhs[t, part], img(2 * t + kh, src), NN)
                g[part, lanes] = total

        def centre(i, carry):
            rows = own_rows(h * mid + i)
            block = g[rows]
            g[rows] = block - jnp.mean(block, axis=1, keepdims=True)
            return carry

        lax.fori_loop(0, mid, centre, 0)

    fan = w.shape[1]
    cols = (slice(0, fan // 2), slice(fan // 2, fan))

    def up_copy(b, k):
        at = (own_rows(b), cols[k])
        return rc(up_out.at[at], up_in.at[at], gu_send.at[b, k], gu_recv.at[b, k], below)

    def dn_copy(b, k):
        at = (own_rows(b), cols[k])
        return rc(dn_out.at[at], dn_in.at[at], gd_send.at[b, k], gd_recv.at[b, k], above)

    def first_up(b):
        for k in range(2):
            at = (own_rows(b), cols[k])
            up_out[at] = g[at].astype(BF)
            up_copy(b, k).start()

    def first_dn(b):
        for k in range(2):
            at = (own_rows(b), cols[k])
            dn_out[at] = g[at].astype(BF)
            dn_copy(b, k).start()

    for turn in range(2):
        if turn == 1:
            filters_step(tall - 1)
        h = own_half if turn == 0 else 1 - own_half

        def step(t, carry):
            forward(h, t)
            return carry

        lax.fori_loop(0, WIDE, step, 0)
        filter_terms(h)

        @pl.when(r == 0)
        def _():
            for i in range(mid):
                b = turn * mid + mid - 1 - i
                if b > 0:
                    first_up(b)

        @pl.when(r == tall - 1)
        def _():
            for i in range(mid):
                b = (1 - turn) * mid + i
                if b < tall - 1:
                    first_dn(b)

    def relay(step):
        b_up = tall - 1 - (step - r)
        b_dn = step - (tall - 1 - r)

        @pl.when((r > 0) & (b_up <= tall - 1) & (b_up > r))
        def _():
            for k in range(2):
                at = (own_rows(b_up), cols[k])
                wait_in(up_in.at[at], gu_recv.at[b_up, k])
                up_out[at] = (g[at] + up_in[at].astype(F32)).astype(BF)
                up_copy(b_up, k).start()

        @pl.when((r < tall - 1) & (b_dn >= 0) & (b_dn < r))
        def _():
            for k in range(2):
                at = (own_rows(b_dn), cols[k])
                wait_in(dn_in.at[at], gd_recv.at[b_dn, k])
                dn_out[at] = (g[at] + dn_in[at].astype(F32)).astype(BF)
                dn_copy(b_dn, k).start()

    def taps(t, kh):
        c = kh * three
        even = dot(gy[t], w[:, c + one : c + two], NN)
        odd = dot(gy[t], w[:, c + two : c + three], NN)
        odd += dot(gys[t], w[:, c : c + one], NN)
        return even, odd

    def tile_row(t, row):
        if row == 0:
            return taps(t, 1)
        even, odd = taps(t, 2)
        more_even, more_odd = taps(t + 1, 0)
        return even + more_even, odd + more_odd

    halves = (slice(0, one), slice(one, two))
    rim_pc = rc(rim_s, rim_p, e_send, e_recv.at[0], p)
    rim_qc = rc(rim_s, rim_q, e_send, e_recv.at[1], q)
    rim_zc = rc(rim_s, rim_z, e_send, e_recv.at[2], above)

    @pl.when(r > 0)
    def _():
        edge = taps(0, 0)
        for part, lanes in zip(edge, halves):
            acc[0, :, lanes] = part

        @pl.when(f % 2 == 0)
        def _():
            rim_s[...] = acc[0].astype(BF)
            rim_pc.start()

    def p_copy(k):
        return rc(to_p.at[k], from_p.at[k], d_send.at[k], d_recv.at[k], p)

    for k in (1, 0):
        t = fd if k else fp
        for row in range(2):
            for part, lanes in zip(tile_row(t, row), halves):
                to_p[k, row, :, lanes] = part.astype(BF)
        p_copy(k).start()

    @pl.when((r > 0) & (f == 1))
    def _():
        wait_in(rim_p, e_recv.at[0])
        rim_s[...] = (acc[0] + rim_p[...].astype(F32)).astype(BF)
        rim_qc.start()

    @pl.when((r > 0) & (f == 3))
    def _():
        wait_in(rim_p, e_recv.at[0])
        wait_in(rim_q, e_recv.at[1])
        rim_s[...] = (acc[0] + rim_p[...].astype(F32) + rim_q[...].astype(F32)).astype(BF)
        rim_zc.start()

    relay(1)
    q_copy = rc(to_q, from_q, d_send.at[2], d_recv.at[2], q)
    wait_in(from_p.at[1], d_recv.at[1])
    for row in range(2):
        for part, lanes in zip(tile_row(fq, row), halves):
            to_q[row, :, lanes] = (part + from_p[1, row, :, lanes].astype(F32)).astype(BF)
    q_copy.start()
    for step in range(2, tall - 1):
        relay(step)
    for row in range(2):
        for part, lanes in zip(tile_row(f, row), halves):
            acc[row, :, lanes] = part

    wait_in(from_p.at[0], d_recv.at[0])
    wait_in(from_q, d_recv.at[2])
    for row in range(2):
        acc[row] += from_p[0, row].astype(F32) + from_q[row].astype(F32)

    @pl.when((r < tall - 1) & (f == 3))
    def _():
        wait_in(rim_z, e_recv.at[2])
        acc[1] += rim_z[...].astype(F32)

    for row in range(2):
        dout[:, row] = acc[row].astype(BF).reshape(imgs, half, two)

    gout[...] = g[own_rows(r)]

    @pl.when(r > 0)
    def _():
        for k in range(2):
            wait_in(up_in.at[own_rows(r), cols[k]], gu_recv.at[r, k])
        gout[...] += up_in[own_rows(r)].astype(F32)

    @pl.when(r < tall - 1)
    def _():
        for k in range(2):
            wait_in(dn_in.at[own_rows(r), cols[k]], gd_recv.at[r, k])
        gout[...] += dn_in[own_rows(r)].astype(F32)

    for row in range(2):
        img_copy(row, 0, p).wait_send()
        img_copy(row, 1, q).wait_send()
        fwd_copy(row).wait_send()
    tgt_copy(0, fp, p).wait_send()
    tgt_copy(1, fq, q).wait_send()
    tgt_copy(2, fd, d).wait_send()
    p_copy(0).wait_send()
    p_copy(1).wait_send()
    q_copy.wait_send()

    @pl.when((f == 3) & (r < tall - 1))
    def _():
        rim_in.wait_send()

    @pl.when((r > 0) & (f == 3))
    def _():
        rim_to_q.wait_send()

    @pl.when((r > 0) & (f % 2 == 1))
    def _():
        rim_to_p.wait_send()

    @pl.when(r > 0)
    def _():
        rim_pc.wait_send()

    for b in range(tall):
        @pl.when((r < tall - 1) & (b <= r))
        def _():
            w_copy(b, False, w_up, below).wait_send()

        @pl.when((r > 0) & (b >= r))
        def _():
            w_copy(b, False, w_dn, above).wait_send()

        @pl.when(b > r)
        def _():
            up_copy(b, 0).wait_send()
            up_copy(b, 1).wait_send()

        @pl.when(b < r)
        def _():
            dn_copy(b, 0).wait_send()
            dn_copy(b, 1).wait_send()


def shards(images, target, raw_filters):
    count_img, two_rows, in_cols, cin = images.shape
    half = in_cols // 2
    own = raw_filters.shape[0]
    tall = lax.axis_size("space") // WIDE
    fan = 9 * cin
    px = count_img * half
    filters = tall * own
    own_hat, own_spread = standardize(raw_filters.reshape(own, fan))
    pair = images.reshape(count_img, two_rows, half, 2 * cin)
    goal = target.reshape(px, tall, WIDE, own).transpose(2, 0, 1, 3).reshape(WIDE, px, filters)
    vm = pltpu.VMEM
    dma = pltpu.SemaphoreType.DMA
    row = (px, 2 * cin)
    scratch = [
        vm((2 * WIDE + 1, count_img, half, 2 * cin), BF), vm((filters, fan), BF), vm((WIDE, px, filters), BF),
        vm((WIDE + 1, px, filters), BF), vm((WIDE + 1, px, filters), BF),
        vm((WIDE, filters, px), BF), vm((WIDE, filters, px), BF), vm((filters, fan), F32),
        vm((filters, fan), BF), vm((filters, fan), BF), vm((filters, fan), BF), vm((filters, fan), BF),
        vm((2, 2) + row, BF), vm((2, 2) + row, BF), vm((2,) + row, BF), vm((2,) + row, BF),
        vm((2,) + row, F32), vm(row, BF), vm(row, BF), vm(row, BF), vm(row, BF),
        dma((WIDE, 2)), dma((3, 2)), dma((tall,)), dma((tall,)), dma((tall,)),
        dma((WIDE,)), dma((3,)), dma, dma((3,)),
        dma((tall, 2)), dma((tall, 2)), dma((tall, 2)), dma((tall, 2)), dma((3,)), dma((3,)), dma((3,)), dma,
    ]
    inner, summed = pl.pallas_call(
        functools.partial(kernel, tall, own, half, cin),
        out_shape=(
            jax.ShapeDtypeStruct(pair.shape, BF),
            jax.ShapeDtypeStruct((own, fan), F32),
        ),
        in_specs=[pl.BlockSpec(memory_space=pltpu.VMEM)] * 3,
        out_specs=[pl.BlockSpec(memory_space=pltpu.VMEM)] * 2,
        scratch_shapes=scratch,
        compiler_params=pltpu.CompilerParams(
            collective_id=0, has_side_effects=True, vmem_limit_bytes=60 * 1024 * 1024
        ),
        name="tiles",
    )(pair, goal, own_hat.astype(BF))
    input_grads = inner.reshape(images.shape)
    first_mean = jnp.mean(summed, axis=1, keepdims=True)
    second_mean = jnp.mean(summed * own_hat, axis=1, keepdims=True)
    filter_grads = ((summed - first_mean - own_hat * second_mean) / own_spread).reshape(
        raw_filters.shape
    )
    return (input_grads, filter_grads)


def solution(mesh):
    return jax.shard_map(
        shards,
        mesh=mesh,
        in_specs=(
            P("parts", "space", None, None),
            P("parts", "space", None, None),
            P(("parts", "space"), None, None, None),
        ),
        out_specs=(P("parts", "space", None, None), P(("parts", "space"), None, None, None)),
        check_vma=False,
    )
```

```python
import functools

import jax
import jax.numpy as jnp
from jax import lax
from jax.experimental import pallas as pl
from jax.experimental.pallas import tpu as pltpu
from jax.sharding import PartitionSpec as P

EPS = 1e-05
GRAD_SCALE = 0.015625
WIDE = 4
F32 = jnp.float32
BF = jnp.bfloat16
NT = (((1,), (1,)), ((), ()))
NN = (((1,), (0,)), ((), ()))


def standardize(rows):
    values = rows.astype(F32)
    centre = jnp.mean(values, axis=1, keepdims=True)
    shifted = values - centre
    spread = jnp.sqrt(jnp.mean(shifted * shifted, axis=1, keepdims=True) + EPS)
    return (shifted / spread, spread)


def dot(a, b, dims):
    return lax.dot_general(a, b, dims, preferred_element_type=F32)


def kernel(
    tall, own, half, cin,
    pair, goal, hat, dout, gout,
    x, w, tg, gy, gys, gt, gts, g,
    up_in, dn_in, up_out, dn_out,
    to_p, from_p, to_q, from_q, acc, rim_s, rim_p, rim_q, rim_z,
    x_recv, x_send, w_recv, w_up, w_dn, t_recv, t_send, r_recv, r_send,
    gu_recv, gu_send, gd_recv, gd_send, d_recv, d_send, e_recv, e_send,
):
    me = lax.axis_index("space")
    r, f = me // WIDE, me % WIDE
    base = r * WIDE
    fp = f + 1 - 2 * (f % 2)
    fq = f + 2 - 4 * (f // 2)
    fd = fp + 2 - 4 * (fp // 2)
    p, q, d = base + fp, base + fq, base + fd
    above, below = me - WIDE, me + WIDE
    imgs = pair.shape[0]
    px = imgs * half
    two, one = 2 * cin, cin
    three = 3 * cin

    def rc(src, dst, ssem, rsem, to):
        return pltpu.make_async_remote_copy(
            src_ref=src, dst_ref=dst, send_sem=ssem, recv_sem=rsem,
            device_id={"space": to}, device_id_type=pl.DeviceIdType.MESH,
        )

    def wait_in(dst, rsem):
        rc(dst, dst, rsem, rsem, p).wait_recv()

    bar = pltpu.get_barrier_semaphore()

    def greet(to):
        pl.semaphore_signal(bar, inc=1, device_id={"space": to}, device_id_type=pl.DeviceIdType.MESH)

    for to in (p, q, d):
        greet(to)

    @pl.when(r > 0)
    def _():
        greet(above)

    @pl.when(r < tall - 1)
    def _():
        greet(below)

    inside = (r > 0) & (r < tall - 1)

    @pl.when(inside)
    def _():
        pl.semaphore_wait(bar, 5)

    @pl.when(jnp.logical_not(inside))
    def _():
        pl.semaphore_wait(bar, 4)

    def own_rows(b):
        return pl.ds(pl.multiple_of(b * own, own), own)

    def img_copy(row, k, to):
        slot = x.at[1 + 2 * f + row]
        return rc(pair.at[:, row], slot, x_send.at[k, row], x_recv.at[f, row], to)

    def fwd_copy(row):
        slot = x.at[1 + 2 * fq + row]
        return rc(slot, slot, x_send.at[2, row], x_recv.at[fq, row], p)

    def tgt_copy(k, to_f, to):
        return rc(goal.at[to_f], tg.at[f], t_send.at[k], t_recv.at[f], to)

    def w_copy(b, first, sem, to):
        slot = w.at[own_rows(b)]
        return rc(hat if first else slot, slot, sem.at[b], w_recv.at[b], to)

    rim_in = rc(pair.at[:, 1], x.at[0], r_send.at[0], r_recv, below)
    rim_to_p = rc(x.at[0], x.at[0], r_send.at[1], r_recv, p)
    rim_to_q = rc(x.at[0], x.at[0], r_send.at[2], r_recv, q)

    def filters_step(s):
        b_up, b_dn = r - s, r + s

        @pl.when(b_up >= 0)
        def _():
            if s > 0:
                wait_in(w.at[own_rows(b_up)], w_recv.at[b_up])

            @pl.when(r < tall - 1)
            def _():
                w_copy(b_up, s == 0, w_up, below).start()

        @pl.when(b_dn <= tall - 1)
        def _():
            if s > 0:
                wait_in(w.at[own_rows(b_dn)], w_recv.at[b_dn])

            @pl.when(r > 0)
            def _():
                w_copy(b_dn, s == 0, w_dn, above).start()

    filters_step(0)

    @pl.when((f == 3) & (r < tall - 1))
    def _():
        rim_in.start()

    for row in range(2):
        img_copy(row, 1, q).start()
    for row in range(2):
        img_copy(row, 0, p).start()
    tgt_copy(0, fp, p).start()
    tgt_copy(1, fq, q).start()
    tgt_copy(2, fd, d).start()
    for row in range(2):
        x[1 + 2 * f + row] = pair[:, row]
    w[own_rows(r)] = hat[...]
    tg[f] = goal[f]

    def forward_row(row):
        wait_in(x.at[1 + 2 * fq + row], x_recv.at[fq, row])
        fwd_copy(row).start()

    def rim_step():
        @pl.when(r > 0)
        def _():
            wait_in(x.at[0], r_recv)

            @pl.when(f == 3)
            def _():
                rim_to_q.start()

            @pl.when(f % 2 == 1)
            def _():
                rim_to_p.start()

        @pl.when(r == 0)
        def _():
            x[0] = jnp.zeros((imgs, half, two), BF)

    for s in range(1, tall - 1):
        filters_step(s)
        if s == 1:
            forward_row(0)
            rim_step()
        if s == 2:
            forward_row(1)
    for row in range(2):
        wait_in(x.at[1 + 2 * fp + row], x_recv.at[fp, row])
        wait_in(x.at[1 + 2 * fd + row], x_recv.at[fd, row])
    for t in (fp, fq, fd):
        wait_in(tg.at[t], t_recv.at[t])

    filters = tall * own
    hf, mid = filters // 2, tall // 2
    own_half = r // mid
    place = lax.broadcasted_iota(jnp.int32, (px, hf), 0) % half
    gy[WIDE] = jnp.zeros((px, filters), BF)
    gys[WIDE] = jnp.zeros((px, filters), BF)

    def img(index, lanes):
        return x[index, :, :, lanes].reshape(px, lanes.stop - lanes.start)

    def forward(h, t):
        part = pl.ds(pl.multiple_of(h * hf, hf), hf)
        both = jnp.zeros((px, hf), F32)
        left = jnp.zeros((px, hf), F32)
        for kh in range(3):
            c = kh * three
            both += dot(img(2 * t + kh, slice(0, two)), w[part, c + one : c + three], NT)
            left += dot(img(2 * t + kh, slice(one, two)), w[part, c : c + one], NT)
        out = both + jnp.where(place == 0, 0.0, pltpu.roll(left, 1, 0))
        grad = ((out - tg[t, :, part].astype(F32)) * GRAD_SCALE).astype(BF)
        wide = grad.astype(F32)
        ahead = jnp.where(place == half - 1, 0.0, pltpu.roll(wide, px - 1, 0))
        gy[t, :, part] = grad
        gys[t, :, part] = ahead.astype(BF)
        gt[t, part] = wide.T.astype(BF)
        gts[t, part] = ahead.T.astype(BF)

    def filter_terms(h):
        part = pl.ds(pl.multiple_of(h * hf, hf), hf)
        for kh in range(3):
            c = kh * three
            for n in range(3):
                lanes = slice(c + n * one, c + (n + 1) * one)
                src = slice(0, one) if n == 1 else slice(one, two)
                lhs = gts if n == 0 else gt
                total = dot(lhs[0, part], img(kh, src), NN)
                for t in range(1, WIDE):
                    total += dot(lhs[t, part], img(2 * t + kh, src), NN)
                g[part, lanes] = total

        def centre(i, carry):
            rows = own_rows(h * mid + i)
            block = g[rows]
            g[rows] = block - jnp.mean(block, axis=1, keepdims=True)
            return carry

        lax.fori_loop(0, mid, centre, 0)

    fan = w.shape[1]
    cols = (slice(0, fan // 2), slice(fan // 2, fan))

    def up_copy(b, k):
        at = (own_rows(b), cols[k])
        return rc(up_out.at[at], up_in.at[at], gu_send.at[b, k], gu_recv.at[b, k], below)

    def dn_copy(b, k):
        at = (own_rows(b), cols[k])
        return rc(dn_out.at[at], dn_in.at[at], gd_send.at[b, k], gd_recv.at[b, k], above)

    def first_up(b):
        for k in range(2):
            at = (own_rows(b), cols[k])
            up_out[at] = g[at].astype(BF)
            up_copy(b, k).start()

    def first_dn(b):
        for k in range(2):
            at = (own_rows(b), cols[k])
            dn_out[at] = g[at].astype(BF)
            dn_copy(b, k).start()

    for turn in range(2):
        if turn == 1:
            filters_step(tall - 1)
        h = own_half if turn == 0 else 1 - own_half

        def step(t, carry):
            forward(h, t)
            return carry

        lax.fori_loop(0, WIDE, step, 0)
        filter_terms(h)

        @pl.when(r == 0)
        def _():
            for i in range(mid):
                b = turn * mid + mid - 1 - i
                if b > 0:
                    first_up(b)

        @pl.when(r == tall - 1)
        def _():
            for i in range(mid):
                b = (1 - turn) * mid + i
                if b < tall - 1:
                    first_dn(b)

    def relay(step):
        b_up = tall - 1 - (step - r)
        b_dn = step - (tall - 1 - r)

        @pl.when((r > 0) & (b_up <= tall - 1) & (b_up > r))
        def _():
            for k in range(2):
                at = (own_rows(b_up), cols[k])
                wait_in(up_in.at[at], gu_recv.at[b_up, k])
                up_out[at] = (g[at] + up_in[at].astype(F32)).astype(BF)
                up_copy(b_up, k).start()

        @pl.when((r < tall - 1) & (b_dn >= 0) & (b_dn < r))
        def _():
            for k in range(2):
                at = (own_rows(b_dn), cols[k])
                wait_in(dn_in.at[at], gd_recv.at[b_dn, k])
                dn_out[at] = (g[at] + dn_in[at].astype(F32)).astype(BF)
                dn_copy(b_dn, k).start()

    def taps(t, kh):
        c = kh * three
        even = dot(gy[t], w[:, c + one : c + two], NN)
        odd = dot(gy[t], w[:, c + two : c + three], NN)
        odd += dot(gys[t], w[:, c : c + one], NN)
        return even, odd

    def tile_row(t, row):
        if row == 0:
            return taps(t, 1)
        even, odd = taps(t, 2)
        more_even, more_odd = taps(t + 1, 0)
        return even + more_even, odd + more_odd

    halves = (slice(0, one), slice(one, two))
    rim_pc = rc(rim_s, rim_p, e_send, e_recv.at[0], p)
    rim_qc = rc(rim_s, rim_q, e_send, e_recv.at[1], q)
    rim_zc = rc(rim_s, rim_z, e_send, e_recv.at[2], above)

    @pl.when(r > 0)
    def _():
        edge = taps(0, 0)
        for part, lanes in zip(edge, halves):
            acc[0, :, lanes] = part

        @pl.when(f % 2 == 0)
        def _():
            rim_s[...] = acc[0].astype(BF)
            rim_pc.start()

    def p_copy(k):
        return rc(to_p.at[k], from_p.at[k], d_send.at[k], d_recv.at[k], p)

    for k in (1, 0):
        t = fd if k else fp
        for row in range(2):
            for part, lanes in zip(tile_row(t, row), halves):
                to_p[k, row, :, lanes] = part.astype(BF)
        p_copy(k).start()

    @pl.when((r > 0) & (f == 1))
    def _():
        wait_in(rim_p, e_recv.at[0])
        rim_s[...] = (acc[0] + rim_p[...].astype(F32)).astype(BF)
        rim_qc.start()

    @pl.when((r > 0) & (f == 3))
    def _():
        wait_in(rim_p, e_recv.at[0])
        wait_in(rim_q, e_recv.at[1])
        rim_s[...] = (acc[0] + rim_p[...].astype(F32) + rim_q[...].astype(F32)).astype(BF)
        rim_zc.start()

    relay(1)
    q_copy = rc(to_q, from_q, d_send.at[2], d_recv.at[2], q)
    wait_in(from_p.at[1], d_recv.at[1])
    for row in range(2):
        for part, lanes in zip(tile_row(fq, row), halves):
            to_q[row, :, lanes] = (part + from_p[1, row, :, lanes].astype(F32)).astype(BF)
    q_copy.start()
    for step in range(2, tall - 1):
        relay(step)
    for row in range(2):
        for part, lanes in zip(tile_row(f, row), halves):
            acc[row, :, lanes] = part

    wait_in(from_p.at[0], d_recv.at[0])
    wait_in(from_q, d_recv.at[2])
    for row in range(2):
        acc[row] += from_p[0, row].astype(F32) + from_q[row].astype(F32)

    @pl.when((r < tall - 1) & (f == 3))
    def _():
        wait_in(rim_z, e_recv.at[2])
        acc[1] += rim_z[...].astype(F32)

    for row in range(2):
        dout[:, row] = acc[row].astype(BF).reshape(imgs, half, two)

    gout[...] = g[own_rows(r)]

    @pl.when(r > 0)
    def _():
        for k in range(2):
            wait_in(up_in.at[own_rows(r), cols[k]], gu_recv.at[r, k])
        gout[...] += up_in[own_rows(r)].astype(F32)

    @pl.when(r < tall - 1)
    def _():
        for k in range(2):
            wait_in(dn_in.at[own_rows(r), cols[k]], gd_recv.at[r, k])
        gout[...] += dn_in[own_rows(r)].astype(F32)

    for row in range(2):
        img_copy(row, 0, p).wait_send()
        img_copy(row, 1, q).wait_send()
        fwd_copy(row).wait_send()
    tgt_copy(0, fp, p).wait_send()
    tgt_copy(1, fq, q).wait_send()
    tgt_copy(2, fd, d).wait_send()
    p_copy(0).wait_send()
    p_copy(1).wait_send()
    q_copy.wait_send()

    @pl.when((f == 3) & (r < tall - 1))
    def _():
        rim_in.wait_send()

    @pl.when((r > 0) & (f == 3))
    def _():
        rim_to_q.wait_send()

    @pl.when((r > 0) & (f % 2 == 1))
    def _():
        rim_to_p.wait_send()

    @pl.when(r > 0)
    def _():
        rim_pc.wait_send()

    for b in range(tall):
        @pl.when((r < tall - 1) & (b <= r))
        def _():
            w_copy(b, False, w_up, below).wait_send()

        @pl.when((r > 0) & (b >= r))
        def _():
            w_copy(b, False, w_dn, above).wait_send()

        @pl.when(b > r)
        def _():
            up_copy(b, 0).wait_send()
            up_copy(b, 1).wait_send()

        @pl.when(b < r)
        def _():
            dn_copy(b, 0).wait_send()
            dn_copy(b, 1).wait_send()


def shards(images, target, raw_filters):
    count_img, two_rows, in_cols, cin = images.shape
    half = in_cols // 2
    own = raw_filters.shape[0]
    tall = lax.axis_size("space") // WIDE
    fan = 9 * cin
    px = count_img * half
    filters = tall * own
    own_hat, own_spread = standardize(raw_filters.reshape(own, fan))
    pair = images.reshape(count_img, two_rows, half, 2 * cin)
    goal = target.reshape(px, tall, WIDE, own).transpose(2, 0, 1, 3).reshape(WIDE, px, filters)
    vm = pltpu.VMEM
    dma = pltpu.SemaphoreType.DMA
    row = (px, 2 * cin)
    scratch = [
        vm((2 * WIDE + 1, count_img, half, 2 * cin), BF), vm((filters, fan), BF), vm((WIDE, px, filters), BF),
        vm((WIDE + 1, px, filters), BF), vm((WIDE + 1, px, filters), BF),
        vm((WIDE, filters, px), BF), vm((WIDE, filters, px), BF), vm((filters, fan), F32),
        vm((filters, fan), BF), vm((filters, fan), BF), vm((filters, fan), BF), vm((filters, fan), BF),
        vm((2, 2) + row, BF), vm((2, 2) + row, BF), vm((2,) + row, BF), vm((2,) + row, BF),
        vm((2,) + row, F32), vm(row, BF), vm(row, BF), vm(row, BF), vm(row, BF),
        dma((WIDE, 2)), dma((3, 2)), dma((tall,)), dma((tall,)), dma((tall,)),
        dma((WIDE,)), dma((3,)), dma, dma((3,)),
        dma((tall, 2)), dma((tall, 2)), dma((tall, 2)), dma((tall, 2)), dma((3,)), dma((3,)), dma((3,)), dma,
    ]
    inner, summed = pl.pallas_call(
        functools.partial(kernel, tall, own, half, cin),
        out_shape=(
            jax.ShapeDtypeStruct(pair.shape, BF),
            jax.ShapeDtypeStruct((own, fan), F32),
        ),
        in_specs=[pl.BlockSpec(memory_space=pltpu.VMEM)] * 3,
        out_specs=[pl.BlockSpec(memory_space=pltpu.VMEM)] * 2,
        scratch_shapes=scratch,
        compiler_params=pltpu.CompilerParams(
            collective_id=0, has_side_effects=True, vmem_limit_bytes=60 * 1024 * 1024
        ),
        name="tiles",
    )(pair, goal, own_hat.astype(BF))
    input_grads = inner.reshape(images.shape)
    first_mean = jnp.mean(summed, axis=1, keepdims=True)
    second_mean = jnp.mean(summed * own_hat, axis=1, keepdims=True)
    filter_grads = ((summed - first_mean - own_hat * second_mean) / own_spread).reshape(
        raw_filters.shape
    )
    return (input_grads, filter_grads)


def solution(mesh):
    return jax.shard_map(
        shards,
        mesh=mesh,
        in_specs=(
            P("parts", "space", None, None),
            P("parts", "space", None, None),
            P(("parts", "space"), None, None, None),
        ),
        out_specs=(P("parts", "space", None, None), P(("parts", "space"), None, None, None)),
        check_vma=False,
    )
```
